32 devices in a mesh: dp: 8 (over y, x, core), expert: 4 (over z).
Axes of the slice: x: 2, y: 2, z: 4, core: 2. Of those that a mesh axis runs over, the one named last changes fastest.
Arguments:
- tokens: bfloat16 [4096, 2048], P(('dp', 'expert')), may hold values from -6 to 6
- routes: int32 [4096, 2], P(('dp', 'expert')), may hold values from 0 to 3, all different within a row; in each aligned block of 128 rows (0 to 127, 128 to 255, ...) at most 80 rows name the same one
- gates: float32 [4096, 2], P(('dp', 'expert')), may hold values from 0.2 to 1
- cotangent: bfloat16 [4096, 2048], P(('dp', 'expert')), may hold values from -6 to 6
- w_gate: bfloat16 [4, 2048, 384], P('expert', 'dp'), may hold values from -0.125 to 0.125
- w_up: bfloat16 [4, 2048, 384], P('expert', 'dp'), may hold values from -0.125 to 0.125
- w_down: bfloat16 [4, 384, 2048], P('expert', None, 'dp'), may hold values from -0.3125 to 0.3125
Outputs:
- mixed: bfloat16 [4096, 2048], P(('dp', 'expert'))
- token_grads: bfloat16 [4096, 2048], P(('dp', 'expert'))
- gate_grads: float32 [4096, 2], P(('dp', 'expert'))
- grad_gate: float32 [4, 2048, 384], P('expert', 'dp')
- grad_up: float32 [4, 2048, 384], P('expert', 'dp')
- grad_down: float32 [4, 384, 2048], P('expert', None, 'dp')
The draws below stay inside these ranges and needn't reach their ends.
Inputs may be any that keep to these rules, and one draw needn't show every extreme that they name: `routes`: each row names 2 different experts. Within the 128 rows of one device no expert is named by more than 80 rows, a bound that some expert reaches in some device's rows.
All inputs are finite; a program needn't handle non-finite values.
Results may differ from the reference program's by a relative error of at most 0.015.
Values may be sent and summed in bfloat16 or wider, within the bound.
A program may use at most 64 MiB of HBM per device.

```python
import math
import jax
import jax.numpy as jnp
import numpy as np
from jax import lax

D = 2048
FF = 384
TOP = 2
TOK_DEV = 128
EXPERTS = 4
CAP = 80
TOKENS = 4096
N_DP = 8
N_EXPERT = 4


def level_of(own_key, extent, split, smallest, high):
    level, own = 1.0, jax.random.fold_in(own_key, 6)
    for dim, shards_of in split:
        heights = jnp.exp(jax.random.uniform(jax.random.fold_in(own, dim), (shards_of,), jnp.float32, smallest / len(split), high / len(split)))
        level = level * jnp.repeat(heights, extent[dim] // shards_of).reshape([-1 if axis == dim else 1 for axis in range(len(extent))])
    return level


def routed_block(key, own, number, rows, amount, top, limit, skew):
    sequence = jax.random.permutation(key, amount)
    crowded, usual = portions_of(amount, rows * top, limit, skew, True), portions_of(amount, rows * top, limit, skew, False)
    places = jnp.arange(amount)

    def named(tallies, rotation):
        used = int((tallies > 0).sum())
        fixed = max(1, used // 4)
        shifted = fixed + (places - fixed + rotation * (used - fixed)) % max(1, amount - fixed)
        return jnp.zeros((amount,), jnp.int32).at[sequence[jnp.where(places < fixed, places, shifted)]].set(jnp.asarray(tallies, jnp.int32))

    tallies = jnp.where(number % 4 == 0, named(crowded, number // 4), named(usual, number - number // 4 - 1))
    mixed = jax.random.permutation(jax.random.fold_in(own, 3), amount)
    donor, taker = mixed[0:amount // 2 * 2:2], mixed[1:amount // 2 * 2:2]
    room = jnp.minimum(tallies[donor] - 1, limit - tallies[taker]) // 2
    room = jnp.where((donor == sequence[0]) | (taker == sequence[0]) | (tallies[taker] == 0), 0, jnp.maximum(room, 0))
    shifted = jax.random.randint(jax.random.fold_in(own, 4), (amount // 2,), 0, 1 << 20) % (room + 1)
    tallies = tallies.at[donor].add(-shifted).at[taker].add(shifted)
    members = jnp.searchsorted(jnp.cumsum(tallies), jnp.arange(rows * top), side="right").astype(jnp.int32)
    grid = members.reshape(top, rows).T
    grid = grid[jax.random.permutation(jax.random.fold_in(own, 1), rows)]
    rotation = jax.random.randint(jax.random.fold_in(own, 2), (rows, 1), 0, top)
    return jnp.take_along_axis(grid, (jnp.arange(top)[None, :] + rotation) % top, axis=1)


def portions_of(number_of, total, reach, slope, full):
    loads = [(1 << 20) // math.isqrt(standing ** slope) + 1 for standing in range(1, number_of + 1)]
    largest = reach if full else min(reach, max(-(-total // number_of), total * loads[0] // sum(loads)))
    least = 1 if total - largest >= number_of - 1 else 0
    given, rest = [largest] + [least] * (number_of - 1), total - largest - least * (number_of - 1)
    while rest > 0:
        movable = [i for i in range(1, number_of) if given[i] < largest] or [i for i in range(1, number_of) if given[i] < reach]
        pool, left = sum([loads[i] for i in movable]), rest
        for i in movable:
            extra = min(reach - given[i], max(1, left * loads[i] // pool), rest)
            given[i] = given[i] + extra
            rest = rest - extra
    return np.array(given)


def scatter_about(rng, extent, deviation, bound, shards=(), kind=jnp.bfloat16):
    values = jax.random.normal(rng, extent, jnp.float32) * deviation
    if len(shards) > 0:
        values = level_of(rng, extent, shards, -0.22, 0.18) * values
    return jnp.clip(values, min=-bound, max=bound).astype(kind)


def setup_inputs(seed: int = 0) -> dict:
    key_of = jax.random.split(jax.random.key(seed), 8)
    tokens = scatter_about(key_of[0], (TOKENS, D), 1.0, 6.0, ((0, 32),))
    routes_keys = jax.random.split(jax.random.fold_in(key_of[1], 1), TOKENS // TOK_DEV)
    routes_turns = jax.random.permutation(jax.random.fold_in(key_of[1], 3), TOKENS // TOK_DEV)
    routes = jax.vmap(lambda own, number: routed_block(jax.random.fold_in(key_of[1], 2), own, number, TOK_DEV, EXPERTS, TOP, CAP, 2))(routes_keys, routes_turns).reshape((TOKENS, TOP))
    gates = jnp.clip(0.2 + 0.8 * jax.random.uniform(key_of[2], (TOKENS, TOP), jnp.float32) ** level_of(key_of[2], (TOKENS, TOP), ((0, 32),), -0.2, 0.2), 0.2, 1.0)
    cotangent = scatter_about(key_of[3], (TOKENS, D), 1.0, 6.0, ((0, 32),))
    w_gate = scatter_about(key_of[4], (EXPERTS, D, FF), D ** -0.5, 0.125, ((0, 4), (1, 8)))
    w_up = scatter_about(key_of[5], (EXPERTS, D, FF), D ** -0.5, 0.125, ((0, 4), (1, 8)))
    w_down = scatter_about(key_of[6], (EXPERTS, FF, D), FF ** -0.5, 0.3125, ((0, 4), (2, 8)))
    return dict(tokens=tokens, routes=routes, gates=gates, cotangent=cotangent, w_gate=w_gate, w_up=w_up, w_down=w_down)


def expert_pass(slot_rows, grad_rows, gate_w, up_w, down_w):
    gate_pre = jnp.dot(slot_rows, gate_w, preferred_element_type=jnp.float32)
    up_pre = jnp.dot(slot_rows, up_w, preferred_element_type=jnp.float32)
    sigma = jax.nn.sigmoid(gate_pre)
    swish = gate_pre * sigma
    hidden = (swish * up_pre).astype(jnp.bfloat16)
    expert_out = jnp.dot(hidden, down_w, preferred_element_type=jnp.float32).astype(jnp.bfloat16)
    d_hidden = lax.dot_general(grad_rows, down_w, (((1,), (1,)), ((), ())), preferred_element_type=jnp.float32)
    d_gate = (d_hidden * up_pre * sigma * (1.0 + gate_pre * (1.0 - sigma))).astype(jnp.bfloat16)
    d_up = (d_hidden * swish).astype(jnp.bfloat16)
    entry_grad = lax.dot_general(d_gate, gate_w, (((1,), (1,)), ((), ())), preferred_element_type=jnp.float32)
    entry_grad = entry_grad + lax.dot_general(d_up, up_w, (((1,), (1,)), ((), ())), preferred_element_type=jnp.float32)
    entry_grad = entry_grad.astype(jnp.bfloat16)
    part_gate = lax.dot_general(slot_rows, d_gate, (((0,), (0,)), ((), ())), preferred_element_type=jnp.float32)
    part_up = lax.dot_general(slot_rows, d_up, (((0,), (0,)), ((), ())), preferred_element_type=jnp.float32)
    part_down = lax.dot_general(hidden, grad_rows, (((0,), (0,)), ((), ())), preferred_element_type=jnp.float32)
    return expert_out, entry_grad, part_gate, part_up, part_down


def reference(tokens, routes, gates, cotangent, w_gate, w_up, w_down):
    block_rows = N_EXPERT * TOK_DEV
    entries = block_rows * TOP
    slots = N_EXPERT * CAP
    token_blocks = tokens.reshape(N_DP, block_rows, D)
    route_blocks = routes.reshape(N_DP, entries)
    gate_blocks = gates.reshape(N_DP, entries)
    cot_blocks = cotangent.reshape(N_DP, block_rows, D)

    def per_block(running, block_data):
        block_tokens, block_routes, block_gates, block_cot = block_data
        scaled = (block_gates[:, None] * jnp.repeat(block_cot.astype(jnp.float32), TOP, axis=0)).astype(jnp.bfloat16)

        def per_expert(totals, expert_id):
            out_rows, grad_acc = totals
            chosen = block_routes == expert_id
            where_rows = jnp.nonzero(chosen, size=slots, fill_value=0)[0].astype(jnp.int32)
            live_rows = (jnp.arange(slots, dtype=jnp.int32) < jnp.sum(chosen.astype(jnp.int32))).astype(jnp.float32)
            slot_rows = (block_tokens[where_rows // TOP].astype(jnp.float32) * live_rows[:, None]).astype(jnp.bfloat16)
            grad_rows = (scaled[where_rows].astype(jnp.float32) * live_rows[:, None]).astype(jnp.bfloat16)
            expert_out, entry_grad, part_gate, part_up, part_down = expert_pass(
                slot_rows, grad_rows, w_gate[expert_id], w_up[expert_id], w_down[expert_id])
            out_rows = out_rows.at[where_rows].add(expert_out.astype(jnp.float32) * live_rows[:, None])
            grad_acc = grad_acc.at[where_rows].add(entry_grad.astype(jnp.float32) * live_rows[:, None])
            return (out_rows, grad_acc), (part_gate.astype(jnp.bfloat16), part_up.astype(jnp.bfloat16), part_down.astype(jnp.bfloat16))

        zeros_rows = jnp.zeros((entries, D), jnp.float32)
        (out_rows, grad_acc), partials = lax.scan(per_expert, (zeros_rows, zeros_rows), jnp.arange(EXPERTS, dtype=jnp.int32))
        running = (running[0] + partials[0].astype(jnp.float32),
                   running[1] + partials[1].astype(jnp.float32),
                   running[2] + partials[2].astype(jnp.float32))
        return running, (out_rows, grad_acc)

    start_sums = (jnp.zeros((EXPERTS, D, FF), jnp.float32), jnp.zeros((EXPERTS, D, FF), jnp.float32),
                  jnp.zeros((EXPERTS, FF, D), jnp.float32))
    sums, (out_rows, grad_acc) = lax.scan(per_block, start_sums, (token_blocks, route_blocks, gate_blocks, cot_blocks))
    per_entry = out_rows.reshape(TOKENS, TOP, D)
    mixed = jnp.sum(gates[:, :, None] * per_entry, axis=1).astype(jnp.bfloat16)
    gate_grads = jnp.sum(cotangent.astype(jnp.float32)[:, None, :] * per_entry, axis=2)
    token_grads = jnp.sum(grad_acc.reshape(TOKENS, TOP, D), axis=1).astype(jnp.bfloat16)
    return mixed, token_grads, gate_grads, sums[0], sums[1], sums[2]
```

```python
import functools

import jax
import jax.numpy as jnp
from jax import lax
from jax.experimental import pallas as pl
from jax.experimental.pallas import tpu as pltpu
from jax.sharding import PartitionSpec as P

F32 = jnp.float32
BF16 = jnp.bfloat16


def dot(left, right, dims):
    return lax.dot_general(left, right, (dims, ((), ())), preferred_element_type=F32)


def kernel(
    experts, groups, cap,
    tokens_ref, cot_ref, gates_ref, gates_t_ref, routes_t_ref, w_ref,
    mixed_ref, token_grads_ref, gate_grads_ref, share_ref,
    place_ref, pick_ref, x_out, x_in, g_out, g_in, y_out, y_in, e_out, e_in,
    weights, gate_pre_ref, up_pre_ref, hidden_ref, d_gate_ref, d_up_ref,
    part, pair_in, summed, rs_in,
    a2a_send, a2a_recv, ag_send, fwd_send, ag_recv, pair_send, pair_recv, rs_send, rs_recv,
):
    me = lax.axis_index("expert")
    here = lax.axis_index("dp")
    chips = groups // 2
    chip = here // 2
    core = here % 2
    partner = here + 1 - 2 * core
    rows = tokens_ref.shape[0]
    width = tokens_ref.shape[1]
    shard = w_ref.shape[1]
    slots = experts * cap

    hops = sorted(range(1, experts), key=lambda s: (abs(2 * s - experts), s))
    chip_hops = sorted(range(1, chips), key=lambda s: (abs(2 * s - chips), s))

    barrier = pltpu.get_barrier_semaphore()
    for s in hops:
        pl.semaphore_signal(barrier, inc=1, device_id={"expert": (me + s) % experts})
    for s in chip_hops:
        pl.semaphore_signal(barrier, inc=1, device_id={"dp": (chip + s) % chips * 2 + core})
    pl.semaphore_signal(barrier, inc=1, device_id={"dp": partner})
    pl.semaphore_wait(barrier, len(hops) + len(chip_hops) + 1)

    def shard_of(ref, owner):
        return ref.at[:, pl.ds(pl.multiple_of(owner * shard, shard), shard), :]

    def weight_send(target, sem):
        return pltpu.make_async_remote_copy(
            src_ref=w_ref, dst_ref=shard_of(weights, here),
            send_sem=ag_send.at[sem], recv_sem=ag_recv.at[here],
            device_id={"dp": target},
        )

    def weight_forward(s):
        source = (chip + s) % chips * 2 + core
        return pltpu.make_async_remote_copy(
            src_ref=shard_of(weights, source), dst_ref=shard_of(weights, source),
            send_sem=fwd_send.at[s], recv_sem=ag_recv.at[source],
            device_id={"dp": partner},
        )

    def weight_arrival(source):
        return pltpu.make_async_remote_copy(
            src_ref=w_ref, dst_ref=shard_of(weights, source),
            send_sem=ag_send.at[0], recv_sem=ag_recv.at[source],
            device_id={"dp": partner},
        )

    for s in chip_hops:
        weight_send((chip + s) % chips * 2 + core, s).start()
    weight_send(partner, 0).start()

    def exchange(number, out, into, s):
        target = (me + s) % experts
        return pltpu.make_async_remote_copy(
            src_ref=out.at[target], dst_ref=into.at[me],
            send_sem=a2a_send.at[number, s], recv_sem=a2a_recv.at[number, me],
            device_id={"expert": target},
        )

    def arrival(number, out, into, s):
        source = (me + s) % experts
        return pltpu.make_async_remote_copy(
            src_ref=out.at[source], dst_ref=into.at[source],
            send_sem=a2a_send.at[number, s], recv_sem=a2a_recv.at[number, source],
            device_id={"expert": source},
        )

    routes_t = routes_t_ref[...]
    expert_ids = lax.broadcasted_iota(jnp.int32, (experts, rows), 0)
    first = expert_ids == routes_t[0:1]
    second = expert_ids == routes_t[1:2]
    member = jnp.where(first | second, 1.0, 0.0)
    earlier = jnp.where(
        lax.broadcasted_iota(jnp.int32, (rows, rows), 0)
        < lax.broadcasted_iota(jnp.int32, (rows, rows), 1), 1.0, 0.0)
    rank = dot(member.astype(BF16), earlier.astype(BF16), ((1,), (0,)))
    places = lax.broadcasted_iota(jnp.int32, (cap, rows), 0)
    for e in range(experts):
        hit = (rank[e:e + 1].astype(jnp.int32) == places).astype(F32)
        for k in range(2):
            named = (routes_t[k:k + 1] == e).astype(F32)
            pick_ref[e * cap:(e + 1) * cap, k * rows:(k + 1) * rows] = (hit * named).astype(BF16)
        place_ref[e] = (hit * member[e:e + 1]).astype(BF16)

    for s in hops + [0]:
        target = (me + s) % experts
        x_out[target] = dot(place_ref[target], tokens_ref[...], ((1,), (0,))).astype(BF16)
        if s:
            exchange(0, x_out, x_in, s).start()
        else:
            x_in[me] = x_out[me]
    for s in hops + [0]:
        target = (me + s) % experts
        at = pl.ds(pl.multiple_of(target * cap, cap), cap)
        gate = jnp.sum(
            pick_ref[at, 0:rows].astype(F32) * gates_t_ref[0:1]
            + pick_ref[at, rows:2 * rows].astype(F32) * gates_t_ref[1:2],
            axis=1, keepdims=True)
        g_out[target] = (
            gate * dot(place_ref[target], cot_ref[...], ((1,), (0,)))).astype(BF16)
        if s:
            exchange(1, g_out, g_in, s).start()
        else:
            g_in[me] = g_out[me]

    weights[:, pl.ds(pl.multiple_of(here * shard, shard), shard), :] = w_ref[...]
    for s in reversed(chip_hops):
        weight_arrival((chip + s) % chips * 2 + core).wait_recv()
        weight_forward(s).start()
    weight_arrival(partner).wait_recv()
    for s in reversed(chip_hops):
        weight_arrival((chip + s) % chips * 2 + 1 - core).wait_recv()
    for s in hops:
        arrival(0, x_out, x_in, s).wait_recv()

    steps = 2
    per = experts // steps
    tall = per * cap

    @pl.loop(0, steps)
    def _(i):
        at = pl.ds(pl.multiple_of(i * tall, tall), tall)
        x = x_in[pl.ds(i * per, per)].reshape(tall, width)
        gate_pre = dot(x, weights[0], ((1,), (0,)))
        up_pre = dot(x, weights[1], ((1,), (0,)))
        gate_pre_ref[at, :] = gate_pre
        up_pre_ref[at, :] = up_pre
        hidden = (gate_pre * jax.nn.sigmoid(gate_pre) * up_pre).astype(BF16)
        hidden_ref[at, :] = hidden
        y_out[pl.ds(i * per, per)] = dot(hidden, weights[2], ((1,), (1,))).astype(BF16).reshape(
            per, cap, width)

    for s in hops:
        exchange(2, y_out, y_in, s).start()
    y_in[me] = y_out[me]

    for s in hops:
        arrival(1, g_out, g_in, s).wait_recv()

    @pl.loop(0, steps)
    def _(i):
        at = pl.ds(pl.multiple_of(i * tall, tall), tall)
        g = g_in[pl.ds(i * per, per)].reshape(tall, width)
        d_hidden = dot(g, weights[2], ((1,), (0,)))
        gate_pre = gate_pre_ref[at, :]
        up_pre = up_pre_ref[at, :]
        sigma = jax.nn.sigmoid(gate_pre)
        d_gate = (d_hidden * up_pre * sigma * (1.0 + gate_pre * (1.0 - sigma))).astype(BF16)
        d_up = (d_hidden * (gate_pre * sigma)).astype(BF16)
        d_gate_ref[at, :] = d_gate
        d_up_ref[at, :] = d_up
        entry = dot(d_gate, weights[0], ((1,), (1,))) + dot(d_up, weights[1], ((1,), (1,)))
        e_out[pl.ds(i * per, per)] = entry.astype(BF16).reshape(per, cap, width)

    for s in hops:
        exchange(3, e_out, e_in, s).start()
    e_in[me] = e_out[me]

    piece = 256

    @pl.loop(0, width // piece)
    def _(i):
        at = pl.ds(pl.multiple_of(i * piece, piece), piece)
        x = x_in[:, :, at].reshape(slots, piece)
        part[0, at, :] = dot(x, d_gate_ref[...], ((0,), (0,))).astype(BF16)
        part[1, at, :] = dot(x, d_up_ref[...], ((0,), (0,))).astype(BF16)
        g = g_in[:, :, at].reshape(slots, piece)
        part[2, at, :] = dot(g, hidden_ref[...], ((0,), (0,))).astype(BF16)

    def pair_send_of(s):
        target = (chip + s) % chips
        return pltpu.make_async_remote_copy(
            src_ref=shard_of(part, target * 2 + 1 - core), dst_ref=pair_in.at[s],
            send_sem=pair_send.at[s], recv_sem=pair_recv.at[s],
            device_id={"dp": partner},
        )

    def share_send_of(s):
        target = (chip + s) % chips
        return pltpu.make_async_remote_copy(
            src_ref=summed.at[s], dst_ref=rs_in.at[s],
            send_sem=rs_send.at[s], recv_sem=rs_recv.at[s],
            device_id={"dp": target * 2 + core},
        )

    def own_sum(s):
        owner = (chip + s) % chips * 2 + core
        own = part[:, pl.ds(pl.multiple_of(owner * shard, shard), shard), :]
        return own.astype(F32) + pair_in[s].astype(F32)

    for s in chip_hops + [0]:
        pair_send_of(s).start()
    for s in chip_hops:
        pair_send_of(s).wait_recv()
        summed[s] = own_sum(s).astype(BF16)
        share_send_of(s).start()
    pair_send_of(0).wait_recv()
    share_ref[...] = own_sum(0)
    for s in reversed(chip_hops):
        share_send_of(s).wait_recv()
        share_ref[...] += rs_in[s].astype(F32)

    for s in hops:
        arrival(2, y_out, y_in, s).wait_recv()

    @pl.loop(0, width // piece)
    def _(i):
        at = pl.ds(pl.multiple_of(i * piece, piece), piece)
        y = y_in[:, :, at].reshape(slots, piece)
        per_entry = dot(pick_ref[...], y, ((0,), (0,)))
        head, tail = per_entry[:rows], per_entry[rows:]
        mixed_ref[:, at] = (
            gates_ref[:, 0:1] * head + gates_ref[:, 1:2] * tail).astype(BF16)
        cot = cot_ref[:, at].astype(F32)
        sums = jnp.concatenate(
            [jnp.sum(cot * head, axis=1, keepdims=True),
             jnp.sum(cot * tail, axis=1, keepdims=True)], axis=1)
        gate_grads_ref[...] = jnp.where(i == 0, 0.0, gate_grads_ref[...]) + sums

    for s in hops:
        arrival(3, e_out, e_in, s).wait_recv()

    @pl.loop(0, width // piece)
    def _(i):
        at = pl.ds(pl.multiple_of(i * piece, piece), piece)
        y = e_in[:, :, at].reshape(slots, piece)
        per_entry = dot(pick_ref[...], y, ((0,), (0,)))
        token_grads_ref[:, at] = (per_entry[:rows] + per_entry[rows:]).astype(BF16)

    for s in chip_hops:
        weight_send((chip + s) % chips * 2 + core, s).wait_send()
        weight_forward(s).wait_send()
        pair_send_of(s).wait_send()
        share_send_of(s).wait_send()
    weight_send(partner, 0).wait_send()
    pair_send_of(0).wait_send()
    for s in hops:
        exchange(0, x_out, x_in, s).wait_send()
        exchange(1, g_out, g_in, s).wait_send()
        exchange(2, y_out, y_in, s).wait_send()
        exchange(3, e_out, e_in, s).wait_send()


def body(tokens, routes, gates, cotangent, w_gate, w_up, w_down):
    experts = lax.axis_size("expert")
    groups = lax.axis_size("dp")
    rows, width = tokens.shape
    picks = routes.shape[1]
    hidden = w_gate.shape[2]
    shard = w_gate.shape[1]
    cap = max(2, 5 * rows * picks // (4 * experts))
    cap = -(-cap // 16) * 16
    slots = experts * cap
    chips = groups // 2
    stacked = jnp.stack([w_gate[0], w_up[0], w_down[0].T])
    vmem = pl.BlockSpec(memory_space=pltpu.VMEM)
    dma = pltpu.SemaphoreType.DMA
    block = pltpu.VMEM((experts, cap, width), BF16)
    mixed, token_grads, gate_grads, share = pl.pallas_call(
        functools.partial(kernel, experts, groups, cap),
        out_shape=(
            jax.ShapeDtypeStruct((rows, width), BF16),
            jax.ShapeDtypeStruct((rows, width), BF16),
            jax.ShapeDtypeStruct((rows, picks), F32),
            jax.ShapeDtypeStruct((3, shard, hidden), F32),
        ),
        in_specs=[vmem] * 6,
        out_specs=(vmem,) * 4,
        scratch_shapes=[
            pltpu.VMEM((experts, cap, rows), BF16),
            pltpu.VMEM((slots, picks * rows), BF16),
            *([block] * 8),
            pltpu.VMEM((3, width, hidden), BF16),
            pltpu.VMEM((slots, hidden), F32),
            pltpu.VMEM((slots, hidden), F32),
            pltpu.VMEM((slots, hidden), BF16),
            pltpu.VMEM((slots, hidden), BF16),
            pltpu.VMEM((slots, hidden), BF16),
            pltpu.VMEM((3, width, hidden), BF16),
            pltpu.VMEM((chips, 3, shard, hidden), BF16),
            pltpu.VMEM((chips, 3, shard, hidden), BF16),
            pltpu.VMEM((chips, 3, shard, hidden), BF16),
            dma((4, experts)), dma((4, experts)),
            dma((chips,)), dma((chips,)), dma((groups,)),
            dma((chips,)), dma((chips,)), dma((chips,)), dma((chips,)),
        ],
        compiler_params=pltpu.CompilerParams(
            collective_id=0, has_side_effects=True, vmem_limit_bytes=58 * 1024 * 1024
        ),
        name="routed_experts",
    )(tokens, cotangent, gates, gates.T, routes.T, stacked)
    return (mixed, token_grads, gate_grads, share[0][None], share[1][None], share[2].T[None])


def solution(mesh):
    return jax.shard_map(
        body,
        mesh=mesh,
        in_specs=(
            P(("dp", "expert"), None),
            P(("dp", "expert"), None),
            P(("dp", "expert"), None),
            P(("dp", "expert"), None),
            P("expert", "dp", None),
            P("expert", "dp", None),
            P("expert", None, "dp"),
        ),
        out_specs=(
            P(("dp", "expert"), None),
            P(("dp", "expert"), None),
            P(("dp", "expert"), None),
            P("expert", "dp", None),
            P("expert", "dp", None),
            P("expert", None, "dp"),
        ),
        check_vma=False,
    )
```

```python
import functools

import jax
import jax.numpy as jnp
from jax import lax
from jax.experimental import pallas as pl
from jax.experimental.pallas import tpu as pltpu
from jax.sharding import PartitionSpec as P

F32 = jnp.float32
BF16 = jnp.bfloat16


def dot(left, right, dims):
    return lax.dot_general(left, right, (dims, ((), ())), preferred_element_type=F32)


def direct_kernel(
    experts, groups, cap,
    tokens_ref, cot_ref, gates_ref, gates_t_ref, routes_t_ref, w_ref,
    mixed_ref, token_grads_ref, gate_grads_ref, share_ref,
    place_ref, pick_ref, x_out, x_in, g_out, g_in, y_out, y_in, e_out, e_in,
    weights, gate_pre_ref, up_pre_ref, hidden_ref, d_gate_ref, d_up_ref,
    part, pair_in, summed, rs_in,
    a2a_send, a2a_recv, ag_send, fwd_send, ag_recv, pair_send, pair_recv, rs_send, rs_recv,
):
    me = lax.axis_index("expert")
    here = lax.axis_index("dp")
    chips = groups // 2
    chip = here // 2
    core = here % 2
    partner = here + 1 - 2 * core
    rows = tokens_ref.shape[0]
    width = tokens_ref.shape[1]
    shard = w_ref.shape[1]
    slots = experts * cap

    hops = sorted(range(1, experts), key=lambda s: (abs(2 * s - experts), s))
    chip_hops = sorted(range(1, chips), key=lambda s: (abs(2 * s - chips), s))

    barrier = pltpu.get_barrier_semaphore()
    for s in hops:
        pl.semaphore_signal(barrier, inc=1, device_id={"expert": (me + s) % experts})
    for s in chip_hops:
        pl.semaphore_signal(barrier, inc=1, device_id={"dp": (chip + s) % chips * 2 + core})
    pl.semaphore_signal(barrier, inc=1, device_id={"dp": partner})
    pl.semaphore_wait(barrier, len(hops) + len(chip_hops) + 1)

    def shard_of(ref, owner):
        return ref.at[:, pl.ds(pl.multiple_of(owner * shard, shard), shard), :]

    def weight_send(target, sem):
        return pltpu.make_async_remote_copy(
            src_ref=w_ref, dst_ref=shard_of(weights, here),
            send_sem=ag_send.at[sem], recv_sem=ag_recv.at[here],
            device_id={"dp": target},
        )

    def weight_forward(s):
        source = (chip + s) % chips * 2 + core
        return pltpu.make_async_remote_copy(
            src_ref=shard_of(weights, source), dst_ref=shard_of(weights, source),
            send_sem=fwd_send.at[s], recv_sem=ag_recv.at[source],
            device_id={"dp": partner},
        )

    def weight_arrival(source):
        return pltpu.make_async_remote_copy(
            src_ref=w_ref, dst_ref=shard_of(weights, source),
            send_sem=ag_send.at[0], recv_sem=ag_recv.at[source],
            device_id={"dp": partner},
        )

    for s in chip_hops:
        weight_send((chip + s) % chips * 2 + core, s).start()
    weight_send(partner, 0).start()

    def exchange(number, out, into, s):
        target = (me + s) % experts
        return pltpu.make_async_remote_copy(
            src_ref=out.at[target], dst_ref=into.at[me],
            send_sem=a2a_send.at[number, s], recv_sem=a2a_recv.at[number, me],
            device_id={"expert": target},
        )

    def arrival(number, out, into, s):
        source = (me + s) % experts
        return pltpu.make_async_remote_copy(
            src_ref=out.at[source], dst_ref=into.at[source],
            send_sem=a2a_send.at[number, s], recv_sem=a2a_recv.at[number, source],
            device_id={"expert": source},
        )

    routes_t = routes_t_ref[...]
    expert_ids = lax.broadcasted_iota(jnp.int32, (experts, rows), 0)
    first = expert_ids == routes_t[0:1]
    second = expert_ids == routes_t[1:2]
    member = jnp.where(first | second, 1.0, 0.0)
    earlier = jnp.where(
        lax.broadcasted_iota(jnp.int32, (rows, rows), 0)
        < lax.broadcasted_iota(jnp.int32, (rows, rows), 1), 1.0, 0.0)
    rank = dot(member.astype(BF16), earlier.astype(BF16), ((1,), (0,)))
    places = lax.broadcasted_iota(jnp.int32, (cap, rows), 0)
    for e in range(experts):
        hit = (rank[e:e + 1].astype(jnp.int32) == places).astype(F32)
        for k in range(2):
            named = (routes_t[k:k + 1] == e).astype(F32)
            pick_ref[e * cap:(e + 1) * cap, k * rows:(k + 1) * rows] = (hit * named).astype(BF16)
        place_ref[e] = (hit * member[e:e + 1]).astype(BF16)

    for s in hops + [0]:
        target = (me + s) % experts
        x_out[target] = dot(place_ref[target], tokens_ref[...], ((1,), (0,))).astype(BF16)
        if s:
            exchange(0, x_out, x_in, s).start()
        else:
            x_in[me] = x_out[me]
    for s in hops + [0]:
        target = (me + s) % experts
        at = pl.ds(pl.multiple_of(target * cap, cap), cap)
        gate = jnp.sum(
            pick_ref[at, 0:rows].astype(F32) * gates_t_ref[0:1]
            + pick_ref[at, rows:2 * rows].astype(F32) * gates_t_ref[1:2],
            axis=1, keepdims=True)
        g_out[target] = (
            gate * dot(place_ref[target], cot_ref[...], ((1,), (0,)))).astype(BF16)
        if s:
            exchange(1, g_out, g_in, s).start()
        else:
            g_in[me] = g_out[me]

    weights[:, pl.ds(pl.multiple_of(here * shard, shard), shard), :] = w_ref[...]
    for s in reversed(chip_hops):
        weight_arrival((chip + s) % chips * 2 + core).wait_recv()
        weight_forward(s).start()
    weight_arrival(partner).wait_recv()
    for s in reversed(chip_hops):
        weight_arrival((chip + s) % chips * 2 + 1 - core).wait_recv()
    for s in hops:
        arrival(0, x_out, x_in, s).wait_recv()

    steps = 2
    per = experts // steps
    tall = per * cap

    @pl.loop(0, steps)
    def _(i):
        at = pl.ds(pl.multiple_of(i * tall, tall), tall)
        x = x_in[pl.ds(i * per, per)].reshape(tall, width)
        gate_pre = dot(x, weights[0], ((1,), (0,)))
        up_pre = dot(x, weights[1], ((1,), (0,)))
        gate_pre_ref[at, :] = gate_pre
        up_pre_ref[at, :] = up_pre
        hidden = (gate_pre * jax.nn.sigmoid(gate_pre) * up_pre).astype(BF16)
        hidden_ref[at, :] = hidden
        y_out[pl.ds(i * per, per)] = dot(hidden, weights[2], ((1,), (1,))).astype(BF16).reshape(
            per, cap, width)

    for s in hops:
        exchange(2, y_out, y_in, s).start()
    y_in[me] = y_out[me]

    for s in hops:
        arrival(1, g_out, g_in, s).wait_recv()

    @pl.loop(0, steps)
    def _(i):
        at = pl.ds(pl.multiple_of(i * tall, tall), tall)
        g = g_in[pl.ds(i * per, per)].reshape(tall, width)
        d_hidden = dot(g, weights[2], ((1,), (0,)))
        gate_pre = gate_pre_ref[at, :]
        up_pre = up_pre_ref[at, :]
        sigma = jax.nn.sigmoid(gate_pre)
        d_gate = (d_hidden * up_pre * sigma * (1.0 + gate_pre * (1.0 - sigma))).astype(BF16)
        d_up = (d_hidden * (gate_pre * sigma)).astype(BF16)
        d_gate_ref[at, :] = d_gate
        d_up_ref[at, :] = d_up
        entry = dot(d_gate, weights[0], ((1,), (1,))) + dot(d_up, weights[1], ((1,), (1,)))
        e_out[pl.ds(i * per, per)] = entry.astype(BF16).reshape(per, cap, width)

    for s in hops:
        exchange(3, e_out, e_in, s).start()
    e_in[me] = e_out[me]

    piece = 256

    @pl.loop(0, width // piece)
    def _(i):
        at = pl.ds(pl.multiple_of(i * piece, piece), piece)
        x = x_in[:, :, at].reshape(slots, piece)
        part[0, at, :] = dot(x, d_gate_ref[...], ((0,), (0,))).astype(BF16)
        part[1, at, :] = dot(x, d_up_ref[...], ((0,), (0,))).astype(BF16)
        g = g_in[:, :, at].reshape(slots, piece)
        part[2, at, :] = dot(g, hidden_ref[...], ((0,), (0,))).astype(BF16)

    def pair_send_of(s):
        target = (chip + s) % chips
        return pltpu.make_async_remote_copy(
            src_ref=shard_of(part, target * 2 + 1 - core), dst_ref=pair_in.at[s],
            send_sem=pair_send.at[s], recv_sem=pair_recv.at[s],
            device_id={"dp": partner},
        )

    def share_send_of(s):
        target = (chip + s) % chips
        return pltpu.make_async_remote_copy(
            src_ref=summed.at[s], dst_ref=rs_in.at[s],
            send_sem=rs_send.at[s], recv_sem=rs_recv.at[s],
            device_id={"dp": target * 2 + core},
        )

    def own_sum(s):
        owner = (chip + s) % chips * 2 + core
        own = part[:, pl.ds(pl.multiple_of(owner * shard, shard), shard), :]
        return own.astype(F32) + pair_in[s].astype(F32)

    for s in chip_hops + [0]:
        pair_send_of(s).start()
    for s in chip_hops:
        pair_send_of(s).wait_recv()
        summed[s] = own_sum(s).astype(BF16)
        share_send_of(s).start()
    pair_send_of(0).wait_recv()
    share_ref[...] = own_sum(0)
    for s in reversed(chip_hops):
        share_send_of(s).wait_recv()
        share_ref[...] += rs_in[s].astype(F32)

    for s in hops:
        arrival(2, y_out, y_in, s).wait_recv()

    @pl.loop(0, width // piece)
    def _(i):
        at = pl.ds(pl.multiple_of(i * piece, piece), piece)
        y = y_in[:, :, at].reshape(slots, piece)
        per_entry = dot(pick_ref[...], y, ((0,), (0,)))
        head, tail = per_entry[:rows], per_entry[rows:]
        mixed_ref[:, at] = (
            gates_ref[:, 0:1] * head + gates_ref[:, 1:2] * tail).astype(BF16)
        cot = cot_ref[:, at].astype(F32)
        sums = jnp.concatenate(
            [jnp.sum(cot * head, axis=1, keepdims=True),
             jnp.sum(cot * tail, axis=1, keepdims=True)], axis=1)
        gate_grads_ref[...] = jnp.where(i == 0, 0.0, gate_grads_ref[...]) + sums

    for s in hops:
        arrival(3, e_out, e_in, s).wait_recv()

    @pl.loop(0, width // piece)
    def _(i):
        at = pl.ds(pl.multiple_of(i * piece, piece), piece)
        y = e_in[:, :, at].reshape(slots, piece)
        per_entry = dot(pick_ref[...], y, ((0,), (0,)))
        token_grads_ref[:, at] = (per_entry[:rows] + per_entry[rows:]).astype(BF16)

    for s in chip_hops:
        weight_send((chip + s) % chips * 2 + core, s).wait_send()
        weight_forward(s).wait_send()
        pair_send_of(s).wait_send()
        share_send_of(s).wait_send()
    weight_send(partner, 0).wait_send()
    pair_send_of(0).wait_send()
    for s in hops:
        exchange(0, x_out, x_in, s).wait_send()
        exchange(1, g_out, g_in, s).wait_send()
        exchange(2, y_out, y_in, s).wait_send()
        exchange(3, e_out, e_in, s).wait_send()


def direct_body(tokens, routes, gates, cotangent, w_gate, w_up, w_down):
    experts = lax.axis_size("expert")
    groups = lax.axis_size("dp")
    rows, width = tokens.shape
    picks = routes.shape[1]
    hidden = w_gate.shape[2]
    shard = w_gate.shape[1]
    cap = max(2, 5 * rows * picks // (4 * experts))
    cap = -(-cap // 16) * 16
    slots = experts * cap
    chips = groups // 2
    stacked = jnp.stack([w_gate[0], w_up[0], w_down[0].T])
    vmem = pl.BlockSpec(memory_space=pltpu.VMEM)
    dma = pltpu.SemaphoreType.DMA
    block = pltpu.VMEM((experts, cap, width), BF16)
    mixed, token_grads, gate_grads, share = pl.pallas_call(
        functools.partial(direct_kernel, experts, groups, cap),
        out_shape=(
            jax.ShapeDtypeStruct((rows, width), BF16),
            jax.ShapeDtypeStruct((rows, width), BF16),
            jax.ShapeDtypeStruct((rows, picks), F32),
            jax.ShapeDtypeStruct((3, shard, hidden), F32),
        ),
        in_specs=[vmem] * 6,
        out_specs=(vmem,) * 4,
        scratch_shapes=[
            pltpu.VMEM((experts, cap, rows), BF16),
            pltpu.VMEM((slots, picks * rows), BF16),
            *([block] * 8),
            pltpu.VMEM((3, width, hidden), BF16),
            pltpu.VMEM((slots, hidden), F32),
            pltpu.VMEM((slots, hidden), F32),
            pltpu.VMEM((slots, hidden), BF16),
            pltpu.VMEM((slots, hidden), BF16),
            pltpu.VMEM((slots, hidden), BF16),
            pltpu.VMEM((3, width, hidden), BF16),
            pltpu.VMEM((chips, 3, shard, hidden), BF16),
            pltpu.VMEM((chips, 3, shard, hidden), BF16),
            pltpu.VMEM((chips, 3, shard, hidden), BF16),
            dma((4, experts)), dma((4, experts)),
            dma((chips,)), dma((chips,)), dma((groups,)),
            dma((chips,)), dma((chips,)), dma((chips,)), dma((chips,)),
        ],
        compiler_params=pltpu.CompilerParams(
            collective_id=0, has_side_effects=True, vmem_limit_bytes=58 * 1024 * 1024
        ),
        name="routed_experts",
    )(tokens, cotangent, gates, gates.T, routes.T, stacked)
    return (mixed, token_grads, gate_grads, share[0][None], share[1][None], share[2].T[None])


def relay_kernel(
    cap,
    tokens_ref, cot_ref, gates_ref, meta_ref, wg_ref, wu_ref, wd_ref,
    mixed_ref, token_grads_ref, gate_grads_ref, share_g_ref, share_u_ref, share_d_ref,
    pick_ref, relay_pick, meta_in, raw_x, raw_g, x_buddy, g_buddy, x_fw, g_fw, x_in, g_in,
    y_out, e_out, y_near, e_near, y_far, e_far, y_part, e_part, y_mix, e_mix, gg_out, gg_in,
    weights, gate_pre_ref, up_pre_ref, hidden_ref, d_gate_ref, d_up_ref,
    part, pair_in, summed, rs_in,
    raw_send, raw_recv, meta_send, meta_recv, near_send, near_recv, fw_send, fw_recv,
    far_send, far_recv, mix_send, mix_recv, gg_send, gg_recv,
    ag_send, fwd_send, ag_recv, pair_send, pair_recv, rs_send, rs_recv,
):
    experts = 4
    me = lax.axis_index("expert")
    here = lax.axis_index("dp")
    chips = pair_in.shape[0]
    chip = here // 2
    core = here % 2
    partner = here + 1 - 2 * core
    rows = tokens_ref.shape[0]
    width = tokens_ref.shape[1]
    shard = wg_ref.shape[0]
    slots = experts * cap
    half = me // 2
    side = me % 2
    buddy = me + 1 - 2 * side
    base = 2 * half
    far_base = 2 - base
    far = 2 - half
    inner = (me == 1) | (me == 2)
    outer = (me == 0) | (me == 3)
    chip_hops = sorted(range(1, chips), key=lambda s: (abs(2 * s - chips), s))
    gg_hops = (2, 1, 3)

    barrier = pltpu.get_barrier_semaphore()
    for s in gg_hops:
        pl.semaphore_signal(barrier, inc=1, device_id={"expert": (me + s) % experts})
    for s in chip_hops:
        pl.semaphore_signal(barrier, inc=1, device_id={"dp": (chip + s) % chips * 2 + core})
    pl.semaphore_signal(barrier, inc=1, device_id={"dp": partner})

    mine = pl.ds(pl.multiple_of(here * shard, shard), shard)
    weights[0, mine, :] = wg_ref[...]
    weights[1, mine, :] = wu_ref[...]
    weights[2, mine, :] = wd_ref[...].T
    pl.semaphore_wait(barrier, len(gg_hops) + len(chip_hops) + 1)

    def copy(src, dst, send, recv, **to):
        return pltpu.make_async_remote_copy(
            src_ref=src, dst_ref=dst, send_sem=send, recv_sem=recv, device_id=to)

    def shard_of(ref, owner):
        return ref.at[:, pl.ds(pl.multiple_of(owner * shard, shard), shard), :]

    def weight_send(target, sem):
        return copy(shard_of(weights, here), shard_of(weights, here),
                    ag_send.at[sem], ag_recv.at[here], dp=target)

    def weight_forward(s):
        source = (chip + s) % chips * 2 + core
        return copy(shard_of(weights, source), shard_of(weights, source),
                    fwd_send.at[s], ag_recv.at[source], dp=partner)

    def weight_arrival(source):
        return copy(shard_of(weights, here), shard_of(weights, source),
                    ag_send.at[0], ag_recv.at[source], dp=partner)

    def raw_copy(number):
        return copy((tokens_ref, cot_ref)[number], (raw_x, raw_g)[number].at[side],
                    raw_send.at[number], raw_recv.at[number, side], expert=far)

    def raw_arrival(number, q):
        return copy((tokens_ref, cot_ref)[number], (raw_x, raw_g)[number].at[q],
                    raw_send.at[number], raw_recv.at[number, q], expert=far)

    def meta_copy():
        return copy(meta_ref, meta_in.at[side], meta_send, meta_recv.at[side], expert=far)

    def meta_arrival(q):
        return copy(meta_ref, meta_in.at[q], meta_send, meta_recv.at[q], expert=far)

    def near_copy(number):
        src = (x_buddy, g_buddy, y_out.at[buddy], e_out.at[buddy])[number]
        dst = (x_in.at[me], g_in.at[me], y_near.at[side], e_near.at[side])[number]
        return copy(src, dst, near_send.at[number], near_recv.at[number], expert=buddy)

    def near_arrival(number):
        src = (x_buddy, g_buddy, y_out.at[buddy], e_out.at[buddy])[number]
        dst = (x_in.at[buddy], g_in.at[buddy], y_near.at[1 - side], e_near.at[1 - side])[number]
        return copy(src, dst, near_send.at[number], near_recv.at[number], expert=buddy)

    def fw_copy(number, q):
        return copy((x_fw, g_fw)[number].at[q], (x_in, g_in)[number].at[far_base + q],
                    fw_send.at[number, q], fw_recv.at[number, q], expert=buddy)

    def far_copy(number, q):
        return copy((y_out, e_out)[number].at[far_base + q], (y_far, e_far)[number].at[q, side],
                    far_send.at[number, q], far_recv.at[number, q], expert=buddy)

    def far_arrival(number, q):
        return copy((y_out, e_out)[number].at[far_base + q],
                    (y_far, e_far)[number].at[q, 1 - side],
                    far_send.at[number, q], far_recv.at[number, q], expert=buddy)

    def mix_copy(number, q):
        return copy((y_part, e_part)[number].at[q], (y_mix, e_mix)[number],
                    mix_send.at[number, q], mix_recv.at[number], expert=far_base + q)

    def gg_copy(s):
        target = (me + s) % experts
        return copy(gg_out.at[target], gg_in.at[me], gg_send.at[s], gg_recv.at[me], expert=target)

    def gg_arrival(s):
        source = (me + s) % experts
        return copy(gg_out.at[source], gg_in.at[source], gg_send.at[s], gg_recv.at[source],
                    expert=source)

    meta_copy().start()
    raw_copy(0).start()
    for s in chip_hops:
        weight_send((chip + s) % chips * 2 + core, s).start()
    weight_send(partner, 0).start()

    earlier = jnp.where(
        lax.broadcasted_iota(jnp.int32, (rows, rows), 0)
        < lax.broadcasted_iota(jnp.int32, (rows, rows), 1), 1.0, 0.0).astype(BF16)
    places = lax.broadcasted_iota(jnp.int32, (cap, rows), 0)

    def picks_of(meta, e):
        first = (meta[0:1].astype(jnp.int32) == e).astype(F32)
        second = (meta[1:2].astype(jnp.int32) == e).astype(F32)
        member = jnp.broadcast_to(first + second, (8, rows))
        rank = dot(member.astype(BF16), earlier, ((1,), (0,)))
        hit = (rank[0:1].astype(jnp.int32) == places).astype(F32)
        return hit * first, hit * second

    def gate_rows(meta, one, two):
        return jnp.sum(one * meta[2:3] + two * meta[3:4], axis=1, keepdims=True)

    meta = meta_ref[...]
    for e in range(experts):
        one, two = picks_of(meta, e)
        pick_ref[e * cap:(e + 1) * cap, 0:rows] = one.astype(BF16)
        pick_ref[e * cap:(e + 1) * cap, rows:2 * rows] = two.astype(BF16)

    def home_picks(e):
        at = pl.ds(pl.multiple_of(e * cap, cap), cap)
        return pick_ref[at, 0:rows].astype(F32), pick_ref[at, rows:2 * rows].astype(F32)

    one, two = home_picks(buddy)
    place = (one + two).astype(BF16)
    x_buddy[...] = dot(place, tokens_ref[...], ((1,), (0,))).astype(BF16)
    near_copy(0).start()
    raw_copy(1).start()
    g_buddy[...] = (
        gate_rows(meta, one, two) * dot(place, cot_ref[...], ((1,), (0,)))).astype(BF16)
    near_copy(1).start()
    one, two = home_picks(me)
    place = (one + two).astype(BF16)
    x_in[me] = dot(place, tokens_ref[...], ((1,), (0,))).astype(BF16)
    g_in[me] = (
        gate_rows(meta, one, two) * dot(place, cot_ref[...], ((1,), (0,)))).astype(BF16)

    def forward_weights(s):
        weight_arrival((chip + s) % chips * 2 + core).wait_recv()
        weight_forward(s).start()

    def relay_x(q):
        meta_arrival(q).wait_recv()
        theirs = meta_in[q]
        at_buddy = pl.ds(pl.multiple_of((1 - side) * cap, cap), cap)
        at_mine = pl.ds(pl.multiple_of(side * cap, cap), cap)
        raw_arrival(0, q).wait_recv()
        one, two = picks_of(theirs, buddy)
        relay_pick[q, at_buddy, 0:rows] = one.astype(BF16)
        relay_pick[q, at_buddy, rows:2 * rows] = two.astype(BF16)
        x_fw[q] = dot((one + two).astype(BF16), raw_x[q], ((1,), (0,))).astype(BF16)
        fw_copy(0, q).start()
        one, two = picks_of(theirs, me)
        relay_pick[q, at_mine, 0:rows] = one.astype(BF16)
        relay_pick[q, at_mine, rows:2 * rows] = two.astype(BF16)
        x_in[far_base + q] = dot((one + two).astype(BF16), raw_x[q], ((1,), (0,))).astype(BF16)

    def relay_g(q):
        theirs = meta_in[q]
        raw_arrival(1, q).wait_recv()
        for l, own in ((1 - side, False), (side, True)):
            at = pl.ds(pl.multiple_of(l * cap, cap), cap)
            one = relay_pick[q, at, 0:rows].astype(F32)
            two = relay_pick[q, at, rows:2 * rows].astype(F32)
            packed = (gate_rows(theirs, one, two)
                      * dot((one + two).astype(BF16), raw_g[q], ((1,), (0,)))).astype(BF16)
            if own:
                g_in[far_base + q] = packed
            else:
                g_fw[q] = packed
                fw_copy(1, q).start()

    piece = 256

    def relay_back(number, q):
        far_arrival(number, q).wait_recv()
        blocks = (y_far, e_far)[number]
        blocks[q, side] = (y_out, e_out)[number][far_base + q]
        eye = (lax.broadcasted_iota(jnp.int32, (rows, rows), 0)
               == lax.broadcasted_iota(jnp.int32, (rows, rows), 1)).astype(F32)
        gate_one = jnp.sum(eye * meta_in[q, 2:3], axis=1, keepdims=True)
        gate_two = jnp.sum(eye * meta_in[q, 3:4], axis=1, keepdims=True)

        @pl.loop(0, width // piece)
        def _(i):
            at = pl.ds(pl.multiple_of(i * piece, piece), piece)
            y = blocks[q, :, :, at].reshape(2 * cap, piece)
            per_entry = dot(relay_pick[q], y, ((0,), (0,)))
            head, tail = per_entry[:rows], per_entry[rows:]
            if number == 0:
                head, tail = gate_one * head, gate_two * tail
            (y_part, e_part)[number][q, :, at] = (head + tail).astype(BF16)

        mix_copy(number, q).start()

    forward_weights(chip_hops[-1])

    @pl.when(inner)
    def _():
        relay_x(0)

    for s in chip_hops[:-1]:
        forward_weights(s)

    @pl.when(inner)
    def _():
        relay_x(1)

    weight_arrival(partner).wait_recv()
    for s in reversed(chip_hops):
        weight_arrival((chip + s) % chips * 2 + 1 - core).wait_recv()
    near_arrival(0).wait_recv()

    @pl.when(outer)
    def _():
        for q in range(2):
            fw_copy(0, q).wait_recv()

    steps = 2
    per = experts // steps
    tall = per * cap

    @pl.loop(0, steps)
    def _(i):
        at = pl.ds(pl.multiple_of(i * tall, tall), tall)
        x = x_in[pl.ds(i * per, per)].reshape(tall, width)
        gate_pre = dot(x, weights[0], ((1,), (0,)))
        up_pre = dot(x, weights[1], ((1,), (0,)))
        gate_pre_ref[at, :] = gate_pre
        up_pre_ref[at, :] = up_pre
        hidden = (gate_pre * jax.nn.sigmoid(gate_pre) * up_pre).astype(BF16)
        hidden_ref[at, :] = hidden
        y_out[pl.ds(i * per, per)] = dot(hidden, weights[2], ((1,), (1,))).astype(BF16).reshape(
            per, cap, width)

    @pl.when(outer)
    def _():
        for q in range(2):
            far_copy(0, q).start()

    near_copy(2).start()
    y_near[side] = y_out[me]

    @pl.when(inner)
    def _():
        relay_g(0)
        relay_g(1)
        relay_back(0, 0)
        relay_back(0, 1)

    near_arrival(1).wait_recv()

    @pl.when(outer)
    def _():
        for q in range(2):
            fw_copy(1, q).wait_recv()

    ones = jnp.ones((8, hidden_ref.shape[1]), BF16)

    @pl.loop(0, steps)
    def _(i):
        at = pl.ds(pl.multiple_of(i * tall, tall), tall)
        g = g_in[pl.ds(i * per, per)].reshape(tall, width)
        d_hidden = dot(g, weights[2], ((1,), (0,)))
        gate_pre = gate_pre_ref[at, :]
        up_pre = up_pre_ref[at, :]
        sigma = jax.nn.sigmoid(gate_pre)
        d_gate = (d_hidden * up_pre * sigma * (1.0 + gate_pre * (1.0 - sigma))).astype(BF16)
        d_up = (d_hidden * (gate_pre * sigma)).astype(BF16)
        d_gate_ref[at, :] = d_gate
        d_up_ref[at, :] = d_up
        entry = dot(d_gate, weights[0], ((1,), (1,))) + dot(d_up, weights[1], ((1,), (1,)))
        e_out[pl.ds(i * per, per)] = entry.astype(BF16).reshape(per, cap, width)
        product = hidden_ref[at, :].astype(F32) * d_hidden
        high = product.astype(BF16)
        low = (product - high.astype(F32)).astype(BF16)
        for j in range(per):
            cut = slice(j * cap, (j + 1) * cap)
            gg_out[i * per + j, :, 0:cap] = (
                dot(ones, high[cut], ((1,), (1,))) + dot(ones, low[cut], ((1,), (1,))))

    @pl.when(outer)
    def _():
        for q in range(2):
            far_copy(1, q).start()

    near_copy(3).start()
    for s in gg_hops:
        gg_copy(s).start()
    e_near[side] = e_out[me]
    gg_in[me] = gg_out[me]

    @pl.loop(0, width // piece)
    def _(i):
        at = pl.ds(pl.multiple_of(i * piece, piece), piece)
        x = x_in[:, :, at].reshape(slots, piece)
        part[0, at, :] = dot(x, d_gate_ref[...], ((0,), (0,))).astype(BF16)
        part[1, at, :] = dot(x, d_up_ref[...], ((0,), (0,))).astype(BF16)
        g = g_in[:, :, at].reshape(slots, piece)
        part[2, at, :] = dot(g, hidden_ref[...], ((0,), (0,))).astype(BF16)

    def pair_send_of(s):
        target = (chip + s) % chips
        return copy(shard_of(part, target * 2 + 1 - core), pair_in.at[s],
                    pair_send.at[s], pair_recv.at[s], dp=partner)

    def share_send_of(s):
        return copy(summed.at[s], rs_in.at[s], rs_send.at[s], rs_recv.at[s],
                    dp=(chip + s) % chips * 2 + core)

    def own_sum(s):
        owner = (chip + s) % chips * 2 + core
        own = part[:, pl.ds(pl.multiple_of(owner * shard, shard), shard), :]
        return own.astype(F32) + pair_in[s].astype(F32)

    for s in chip_hops + [0]:
        pair_send_of(s).start()
    for s in chip_hops:
        pair_send_of(s).wait_recv()
        summed[s] = own_sum(s).astype(BF16)
        share_send_of(s).start()

    @pl.when(inner)
    def _():
        relay_back(1, 0)
        relay_back(1, 1)

    for s in gg_hops:
        gg_arrival(s).wait_recv()
    sums = jnp.zeros((8, 2 * rows), F32)
    for e in range(experts):
        row = gg_in[e, :, 0:cap]
        high = row.astype(BF16)
        low = (row - high.astype(F32)).astype(BF16)
        chosen = pick_ref[e * cap:(e + 1) * cap, :]
        sums += dot(high, chosen, ((1,), (0,))) + dot(low, chosen, ((1,), (0,)))
    gate_grads_ref[0:1, :] = sums[0:1, 0:rows] / meta_ref[2:3, :]
    gate_grads_ref[1:2, :] = sums[0:1, rows:2 * rows] / meta_ref[3:4, :]

    near_at = pl.ds(pl.multiple_of(half * (2 * cap), 2 * cap), 2 * cap)
    near_arrival(2).wait_recv()
    mix_copy(0, 0).wait_recv()

    @pl.loop(0, width // piece)
    def _(i):
        at = pl.ds(pl.multiple_of(i * piece, piece), piece)
        y = y_near[:, :, at].reshape(2 * cap, piece)
        per_entry = dot(pick_ref[near_at, :], y, ((0,), (0,)))
        mixed_ref[:, at] = (
            gates_ref[:, 0:1] * per_entry[:rows] + gates_ref[:, 1:2] * per_entry[rows:]
            + y_mix[:, at].astype(F32)).astype(BF16)

    pair_send_of(0).wait_recv()
    total = own_sum(0)
    for s in reversed(chip_hops):
        share_send_of(s).wait_recv()
        total += rs_in[s].astype(F32)
    share_g_ref[...] = total[0]
    share_u_ref[...] = total[1]
    share_d_ref[...] = total[2].T

    near_arrival(3).wait_recv()
    mix_copy(1, 0).wait_recv()

    @pl.loop(0, width // piece)
    def _(i):
        at = pl.ds(pl.multiple_of(i * piece, piece), piece)
        y = e_near[:, :, at].reshape(2 * cap, piece)
        per_entry = dot(pick_ref[near_at, :], y, ((0,), (0,)))
        token_grads_ref[:, at] = (
            per_entry[:rows] + per_entry[rows:] + e_mix[:, at].astype(F32)).astype(BF16)

    meta_copy().wait_send()
    for number in range(2):
        raw_copy(number).wait_send()
    for number in range(4):
        near_copy(number).wait_send()
    for s in gg_hops:
        gg_copy(s).wait_send()
    for s in chip_hops:
        weight_send((chip + s) % chips * 2 + core, s).wait_send()
        weight_forward(s).wait_send()
        pair_send_of(s).wait_send()
        share_send_of(s).wait_send()
    weight_send(partner, 0).wait_send()
    pair_send_of(0).wait_send()

    @pl.when(inner)
    def _():
        for number in range(2):
            for q in range(2):
                fw_copy(number, q).wait_send()
                mix_copy(number, q).wait_send()

    @pl.when(outer)
    def _():
        for number in range(2):
            for q in range(2):
                far_copy(number, q).wait_send()


def relay_body(tokens, routes, gates, cotangent, w_gate, w_up, w_down):
    experts = lax.axis_size("expert")
    groups = lax.axis_size("dp")
    rows, width = tokens.shape
    picks = routes.shape[1]
    hidden = w_gate.shape[2]
    shard = w_gate.shape[1]
    cap = max(2, 5 * rows * picks // (4 * experts))
    cap = -(-cap // 16) * 16
    lanes = -(-cap // 128) * 128
    slots = experts * cap
    chips = groups // 2
    meta = jnp.concatenate(
        [routes.T.astype(F32), gates.T, jnp.zeros((8 - 2 * picks, rows), F32)], axis=0)
    vmem = pl.BlockSpec(memory_space=pltpu.VMEM)
    dma = pltpu.SemaphoreType.DMA
    blocks = lambda *lead: pltpu.VMEM((*lead, cap, width), BF16)
    whole = lambda *lead: pltpu.VMEM((*lead, rows, width), BF16)
    mixed, token_grads, gate_grads, share_g, share_u, share_d = pl.pallas_call(
        functools.partial(relay_kernel, cap),
        out_shape=(
            jax.ShapeDtypeStruct((rows, width), BF16),
            jax.ShapeDtypeStruct((rows, width), BF16),
            jax.ShapeDtypeStruct((picks, rows), F32),
            jax.ShapeDtypeStruct((shard, hidden), F32),
            jax.ShapeDtypeStruct((shard, hidden), F32),
            jax.ShapeDtypeStruct((hidden, shard), F32),
        ),
        in_specs=[vmem] * 7,
        out_specs=(vmem,) * 6,
        scratch_shapes=[
            pltpu.VMEM((slots, picks * rows), BF16),
            pltpu.VMEM((2, 2 * cap, picks * rows), BF16),
            pltpu.VMEM((2, 8, rows), F32),
            whole(2), whole(2),
            blocks(), blocks(), blocks(2), blocks(2),
            blocks(experts), blocks(experts), blocks(experts), blocks(experts),
            blocks(2), blocks(2), blocks(2, 2), blocks(2, 2),
            whole(2), whole(2), whole(), whole(),
            pltpu.VMEM((experts, 8, lanes), F32), pltpu.VMEM((experts, 8, lanes), F32),
            pltpu.VMEM((3, width, hidden), BF16),
            pltpu.VMEM((slots, hidden), F32),
            pltpu.VMEM((slots, hidden), F32),
            pltpu.VMEM((slots, hidden), BF16),
            pltpu.VMEM((slots, hidden), BF16),
            pltpu.VMEM((slots, hidden), BF16),
            pltpu.VMEM((3, width, hidden), BF16),
            pltpu.VMEM((chips, 3, shard, hidden), BF16),
            pltpu.VMEM((chips, 3, shard, hidden), BF16),
            pltpu.VMEM((chips, 3, shard, hidden), BF16),
            dma((2,)), dma((2, 2)), dma(()), dma((2,)), dma((4,)), dma((4,)),
            dma((2, 2)), dma((2, 2)), dma((2, 2)), dma((2, 2)), dma((2, 2)), dma((2,)),
            dma((experts,)), dma((experts,)),
            dma((chips,)), dma((chips,)), dma((groups,)),
            dma((chips,)), dma((chips,)), dma((chips,)), dma((chips,)),
        ],
        compiler_params=pltpu.CompilerParams(
            collective_id=0, has_side_effects=True, vmem_limit_bytes=58 * 1024 * 1024
        ),
        name="routed_experts",
    )(tokens, cotangent, gates, meta, w_gate[0], w_up[0], w_down[0])
    return (mixed, token_grads, gate_grads.T, share_g[None], share_u[None], share_d[None])


def body(*arguments):
    relayed = lax.axis_size("expert") == 4 and arguments[4].shape[1] % 128 == 0
    return (relay_body if relayed else direct_body)(*arguments)


def solution(mesh):
    return jax.shard_map(
        body,
        mesh=mesh,
        in_specs=(
            P(("dp", "expert"), None),
            P(("dp", "expert"), None),
            P(("dp", "expert"), None),
            P(("dp", "expert"), None),
            P("expert", "dp", None),
            P("expert", "dp", None),
            P("expert", None, "dp"),
        ),
        out_specs=(
            P(("dp", "expert"), None),
            P(("dp", "expert"), None),
            P(("dp", "expert"), None),
            P("expert", "dp", None),
            P("expert", "dp", None),
            P("expert", None, "dp"),
        ),
        check_vma=False,
    )
```

```python
import functools

import jax
import jax.numpy as jnp
from jax import lax
from jax.experimental import pallas as pl
from jax.experimental.pallas import tpu as pltpu
from jax.sharding import PartitionSpec as P

F32 = jnp.float32
BF16 = jnp.bfloat16


def dot(left, right, dims):
    return lax.dot_general(left, right, (dims, ((), ())), preferred_element_type=F32)


def direct_kernel(
    experts, groups, cap,
    tokens_ref, cot_ref, gates_ref, gates_t_ref, routes_t_ref, w_ref,
    mixed_ref, token_grads_ref, gate_grads_ref, share_ref,
    place_ref, pick_ref, x_out, x_in, g_out, g_in, y_out, y_in, e_out, e_in,
    weights, gate_pre_ref, up_pre_ref, hidden_ref, d_gate_ref, d_up_ref,
    part, pair_in, summed, rs_in,
    a2a_send, a2a_recv, ag_send, fwd_send, ag_recv, pair_send, pair_recv, rs_send, rs_recv,
):
    me = lax.axis_index("expert")
    here = lax.axis_index("dp")
    chips = groups // 2
    chip = here // 2
    core = here % 2
    partner = here + 1 - 2 * core
    rows = tokens_ref.shape[0]
    width = tokens_ref.shape[1]
    shard = w_ref.shape[1]
    slots = experts * cap

    hops = sorted(range(1, experts), key=lambda s: (abs(2 * s - experts), s))
    chip_hops = sorted(range(1, chips), key=lambda s: (abs(2 * s - chips), s))

    barrier = pltpu.get_barrier_semaphore()
    for s in hops:
        pl.semaphore_signal(barrier, inc=1, device_id={"expert": (me + s) % experts})
    for s in chip_hops:
        pl.semaphore_signal(barrier, inc=1, device_id={"dp": (chip + s) % chips * 2 + core})
    pl.semaphore_signal(barrier, inc=1, device_id={"dp": partner})
    pl.semaphore_wait(barrier, len(hops) + len(chip_hops) + 1)

    def shard_of(ref, owner):
        return ref.at[:, pl.ds(pl.multiple_of(owner * shard, shard), shard), :]

    def weight_send(target, sem):
        return pltpu.make_async_remote_copy(
            src_ref=w_ref, dst_ref=shard_of(weights, here),
            send_sem=ag_send.at[sem], recv_sem=ag_recv.at[here],
            device_id={"dp": target},
        )

    def weight_forward(s):
        source = (chip + s) % chips * 2 + core
        return pltpu.make_async_remote_copy(
            src_ref=shard_of(weights, source), dst_ref=shard_of(weights, source),
            send_sem=fwd_send.at[s], recv_sem=ag_recv.at[source],
            device_id={"dp": partner},
        )

    def weight_arrival(source):
        return pltpu.make_async_remote_copy(
            src_ref=w_ref, dst_ref=shard_of(weights, source),
            send_sem=ag_send.at[0], recv_sem=ag_recv.at[source],
            device_id={"dp": partner},
        )

    for s in chip_hops:
        weight_send((chip + s) % chips * 2 + core, s).start()
    weight_send(partner, 0).start()

    def exchange(number, out, into, s):
        target = (me + s) % experts
        return pltpu.make_async_remote_copy(
            src_ref=out.at[target], dst_ref=into.at[me],
            send_sem=a2a_send.at[number, s], recv_sem=a2a_recv.at[number, me],
            device_id={"expert": target},
        )

    def arrival(number, out, into, s):
        source = (me + s) % experts
        return pltpu.make_async_remote_copy(
            src_ref=out.at[source], dst_ref=into.at[source],
            send_sem=a2a_send.at[number, s], recv_sem=a2a_recv.at[number, source],
            device_id={"expert": source},
        )

    routes_t = routes_t_ref[...]
    expert_ids = lax.broadcasted_iota(jnp.int32, (experts, rows), 0)
    first = expert_ids == routes_t[0:1]
    second = expert_ids == routes_t[1:2]
    member = jnp.where(first | second, 1.0, 0.0)
    earlier = jnp.where(
        lax.broadcasted_iota(jnp.int32, (rows, rows), 0)
        < lax.broadcasted_iota(jnp.int32, (rows, rows), 1), 1.0, 0.0)
    rank = dot(member.astype(BF16), earlier.astype(BF16), ((1,), (0,)))
    places = lax.broadcasted_iota(jnp.int32, (cap, rows), 0)
    for e in range(experts):
        hit = (rank[e:e + 1].astype(jnp.int32) == places).astype(F32)
        for k in range(2):
            named = (routes_t[k:k + 1] == e).astype(F32)
            pick_ref[e * cap:(e + 1) * cap, k * rows:(k + 1) * rows] = (hit * named).astype(BF16)
        place_ref[e] = (hit * member[e:e + 1]).astype(BF16)

    for s in hops + [0]:
        target = (me + s) % experts
        x_out[target] = dot(place_ref[target], tokens_ref[...], ((1,), (0,))).astype(BF16)
        if s:
            exchange(0, x_out, x_in, s).start()
        else:
            x_in[me] = x_out[me]
    for s in hops + [0]:
        target = (me + s) % experts
        at = pl.ds(pl.multiple_of(target * cap, cap), cap)
        gate = jnp.sum(
            pick_ref[at, 0:rows].astype(F32) * gates_t_ref[0:1]
            + pick_ref[at, rows:2 * rows].astype(F32) * gates_t_ref[1:2],
            axis=1, keepdims=True)
        g_out[target] = (
            gate * dot(place_ref[target], cot_ref[...], ((1,), (0,)))).astype(BF16)
        if s:
            exchange(1, g_out, g_in, s).start()
        else:
            g_in[me] = g_out[me]

    weights[:, pl.ds(pl.multiple_of(here * shard, shard), shard), :] = w_ref[...]
    for s in reversed(chip_hops):
        weight_arrival((chip + s) % chips * 2 + core).wait_recv()
        weight_forward(s).start()
    weight_arrival(partner).wait_recv()
    for s in reversed(chip_hops):
        weight_arrival((chip + s) % chips * 2 + 1 - core).wait_recv()
    for s in hops:
        arrival(0, x_out, x_in, s).wait_recv()

    steps = 2
    per = experts // steps
    tall = per * cap

    @pl.loop(0, steps)
    def _(i):
        at = pl.ds(pl.multiple_of(i * tall, tall), tall)
        x = x_in[pl.ds(i * per, per)].reshape(tall, width)
        gate_pre = dot(x, weights[0], ((1,), (0,)))
        up_pre = dot(x, weights[1], ((1,), (0,)))
        gate_pre_ref[at, :] = gate_pre
        up_pre_ref[at, :] = up_pre
        hidden = (gate_pre * jax.nn.sigmoid(gate_pre) * up_pre).astype(BF16)
        hidden_ref[at, :] = hidden
        y_out[pl.ds(i * per, per)] = dot(hidden, weights[2], ((1,), (1,))).astype(BF16).reshape(
            per, cap, width)

    for s in hops:
        exchange(2, y_out, y_in, s).start()
    y_in[me] = y_out[me]

    for s in hops:
        arrival(1, g_out, g_in, s).wait_recv()

    @pl.loop(0, steps)
    def _(i):
        at = pl.ds(pl.multiple_of(i * tall, tall), tall)
        g = g_in[pl.ds(i * per, per)].reshape(tall, width)
        d_hidden = dot(g, weights[2], ((1,), (0,)))
        gate_pre = gate_pre_ref[at, :]
        up_pre = up_pre_ref[at, :]
        sigma = jax.nn.sigmoid(gate_pre)
        d_gate = (d_hidden * up_pre * sigma * (1.0 + gate_pre * (1.0 - sigma))).astype(BF16)
        d_up = (d_hidden * (gate_pre * sigma)).astype(BF16)
        d_gate_ref[at, :] = d_gate
        d_up_ref[at, :] = d_up
        entry = dot(d_gate, weights[0], ((1,), (1,))) + dot(d_up, weights[1], ((1,), (1,)))
        e_out[pl.ds(i * per, per)] = entry.astype(BF16).reshape(per, cap, width)

    for s in hops:
        exchange(3, e_out, e_in, s).start()
    e_in[me] = e_out[me]

    piece = 256

    @pl.loop(0, width // piece)
    def _(i):
        at = pl.ds(pl.multiple_of(i * piece, piece), piece)
        x = x_in[:, :, at].reshape(slots, piece)
        part[0, at, :] = dot(x, d_gate_ref[...], ((0,), (0,))).astype(BF16)
        part[1, at, :] = dot(x, d_up_ref[...], ((0,), (0,))).astype(BF16)
        g = g_in[:, :, at].reshape(slots, piece)
        part[2, at, :] = dot(g, hidden_ref[...], ((0,), (0,))).astype(BF16)

    def pair_send_of(s):
        target = (chip + s) % chips
        return pltpu.make_async_remote_copy(
            src_ref=shard_of(part, target * 2 + 1 - core), dst_ref=pair_in.at[s],
            send_sem=pair_send.at[s], recv_sem=pair_recv.at[s],
            device_id={"dp": partner},
        )

    def share_send_of(s):
        target = (chip + s) % chips
        return pltpu.make_async_remote_copy(
            src_ref=summed.at[s], dst_ref=rs_in.at[s],
            send_sem=rs_send.at[s], recv_sem=rs_recv.at[s],
            device_id={"dp": target * 2 + core},
        )

    def own_sum(s):
        owner = (chip + s) % chips * 2 + core
        own = part[:, pl.ds(pl.multiple_of(owner * shard, shard), shard), :]
        return own.astype(F32) + pair_in[s].astype(F32)

    for s in chip_hops + [0]:
        pair_send_of(s).start()
    for s in chip_hops:
        pair_send_of(s).wait_recv()
        summed[s] = own_sum(s).astype(BF16)
        share_send_of(s).start()
    pair_send_of(0).wait_recv()
    share_ref[...] = own_sum(0)
    for s in reversed(chip_hops):
        share_send_of(s).wait_recv()
        share_ref[...] += rs_in[s].astype(F32)

    for s in hops:
        arrival(2, y_out, y_in, s).wait_recv()

    @pl.loop(0, width // piece)
    def _(i):
        at = pl.ds(pl.multiple_of(i * piece, piece), piece)
        y = y_in[:, :, at].reshape(slots, piece)
        per_entry = dot(pick_ref[...], y, ((0,), (0,)))
        head, tail = per_entry[:rows], per_entry[rows:]
        mixed_ref[:, at] = (
            gates_ref[:, 0:1] * head + gates_ref[:, 1:2] * tail).astype(BF16)
        cot = cot_ref[:, at].astype(F32)
        sums = jnp.concatenate(
            [jnp.sum(cot * head, axis=1, keepdims=True),
             jnp.sum(cot * tail, axis=1, keepdims=True)], axis=1)
        gate_grads_ref[...] = jnp.where(i == 0, 0.0, gate_grads_ref[...]) + sums

    for s in hops:
        arrival(3, e_out, e_in, s).wait_recv()

    @pl.loop(0, width // piece)
    def _(i):
        at = pl.ds(pl.multiple_of(i * piece, piece), piece)
        y = e_in[:, :, at].reshape(slots, piece)
        per_entry = dot(pick_ref[...], y, ((0,), (0,)))
        token_grads_ref[:, at] = (per_entry[:rows] + per_entry[rows:]).astype(BF16)

    for s in chip_hops:
        weight_send((chip + s) % chips * 2 + core, s).wait_send()
        weight_forward(s).wait_send()
        pair_send_of(s).wait_send()
        share_send_of(s).wait_send()
    weight_send(partner, 0).wait_send()
    pair_send_of(0).wait_send()
    for s in hops:
        exchange(0, x_out, x_in, s).wait_send()
        exchange(1, g_out, g_in, s).wait_send()
        exchange(2, y_out, y_in, s).wait_send()
        exchange(3, e_out, e_in, s).wait_send()


def direct_body(tokens, routes, gates, cotangent, w_gate, w_up, w_down):
    experts = lax.axis_size("expert")
    groups = lax.axis_size("dp")
    rows, width = tokens.shape
    picks = routes.shape[1]
    hidden = w_gate.shape[2]
    shard = w_gate.shape[1]
    cap = max(2, 5 * rows * picks // (4 * experts))
    cap = -(-cap // 16) * 16
    slots = experts * cap
    chips = groups // 2
    stacked = jnp.stack([w_gate[0], w_up[0], w_down[0].T])
    vmem = pl.BlockSpec(memory_space=pltpu.VMEM)
    dma = pltpu.SemaphoreType.DMA
    block = pltpu.VMEM((experts, cap, width), BF16)
    mixed, token_grads, gate_grads, share = pl.pallas_call(
        functools.partial(direct_kernel, experts, groups, cap),
        out_shape=(
            jax.ShapeDtypeStruct((rows, width), BF16),
            jax.ShapeDtypeStruct((rows, width), BF16),
            jax.ShapeDtypeStruct((rows, picks), F32),
            jax.ShapeDtypeStruct((3, shard, hidden), F32),
        ),
        in_specs=[vmem] * 6,
        out_specs=(vmem,) * 4,
        scratch_shapes=[
            pltpu.VMEM((experts, cap, rows), BF16),
            pltpu.VMEM((slots, picks * rows), BF16),
            *([block] * 8),
            pltpu.VMEM((3, width, hidden), BF16),
            pltpu.VMEM((slots, hidden), F32),
            pltpu.VMEM((slots, hidden), F32),
            pltpu.VMEM((slots, hidden), BF16),
            pltpu.VMEM((slots, hidden), BF16),
            pltpu.VMEM((slots, hidden), BF16),
            pltpu.VMEM((3, width, hidden), BF16),
            pltpu.VMEM((chips, 3, shard, hidden), BF16),
            pltpu.VMEM((chips, 3, shard, hidden), BF16),
            pltpu.VMEM((chips, 3, shard, hidden), BF16),
            dma((4, experts)), dma((4, experts)),
            dma((chips,)), dma((chips,)), dma((groups,)),
            dma((chips,)), dma((chips,)), dma((chips,)), dma((chips,)),
        ],
        compiler_params=pltpu.CompilerParams(
            collective_id=0, has_side_effects=True, vmem_limit_bytes=58 * 1024 * 1024
        ),
        name="routed_experts",
    )(tokens, cotangent, gates, gates.T, routes.T, stacked)
    return (mixed, token_grads, gate_grads, share[0][None], share[1][None], share[2].T[None])


def line_kernel(
    cap,
    tokens_ref, cot_ref, gates_ref, meta_ref, wg_ref, wu_ref, wd_ref,
    mixed_ref, token_grads_ref, gate_grads_ref, share_g_ref, share_u_ref, share_d_ref,
    pick_ref, x_out, g_out, x_in, g_in,
    y_out, e_out, y_in, e_in, gg_out, gg_in,
    weights, gate_pre_ref, up_pre_ref, hidden_ref, d_gate_ref, d_up_ref,
    part, pair_in, summed, rs_in,
    back_send, back_recv, gg_send, gg_recv,
    ag_send, fwd_send, ag_recv, pair_send, pair_recv, rs_send, rs_recv,
):
    experts = 4
    me = lax.axis_index("expert")
    here = lax.axis_index("dp")
    chips = pair_in.shape[0]
    chip = here // 2
    core = here % 2
    partner = here + 1 - 2 * core
    rows = tokens_ref.shape[0]
    width = tokens_ref.shape[1]
    shard = wg_ref.shape[0]
    slots = experts * cap
    half = me // 2
    side = me % 2
    buddy = me + 1 - 2 * side
    far_base = 2 - 2 * half
    chip_hops = sorted(range(1, chips), key=lambda s: (abs(2 * s - chips), s))
    gg_hops = (2, 1, 3)

    barrier = pltpu.get_barrier_semaphore()
    for s in gg_hops:
        pl.semaphore_signal(barrier, inc=1, device_id={"expert": (me + s) % experts})
    for s in chip_hops:
        pl.semaphore_signal(barrier, inc=1, device_id={"dp": (chip + s) % chips * 2 + core})
    pl.semaphore_signal(barrier, inc=1, device_id={"dp": partner})

    mine = pl.ds(pl.multiple_of(here * shard, shard), shard)
    weights[0, mine, :] = wg_ref[...]
    weights[1, mine, :] = wu_ref[...]
    weights[2, mine, :] = wd_ref[...].T
    pl.semaphore_wait(barrier, len(gg_hops) + len(chip_hops) + 1)

    def copy(src, dst, send, recv, **to):
        return pltpu.make_async_remote_copy(
            src_ref=src, dst_ref=dst, send_sem=send, recv_sem=recv, device_id=to)

    def shard_of(ref, owner):
        return ref.at[:, pl.ds(pl.multiple_of(owner * shard, shard), shard), :]

    def weight_send(target, sem):
        return copy(shard_of(weights, here), shard_of(weights, here),
                    ag_send.at[sem], ag_recv.at[here], dp=target)

    def weight_forward(s):
        source = (chip + s) % chips * 2 + core
        return copy(shard_of(weights, source), shard_of(weights, source),
                    fwd_send.at[s], ag_recv.at[source], dp=partner)

    def weight_arrival(source):
        return copy(shard_of(weights, here), shard_of(weights, source),
                    ag_send.at[0], ag_recv.at[source], dp=partner)

    others = (far_base + side, far_base + 1 - side, buddy)

    def back_copy(number, i):
        return copy((x_out, g_out, y_out, e_out)[number].at[others[i]],
                    (x_in, g_in, y_in, e_in)[number].at[me],
                    back_send.at[number, i], back_recv.at[number, me], expert=others[i])

    def back_arrival(number, i):
        return copy((x_out, g_out, y_out, e_out)[number].at[others[i]],
                    (x_in, g_in, y_in, e_in)[number].at[others[i]],
                    back_send.at[number, i], back_recv.at[number, others[i]], expert=others[i])

    def gg_copy(s):
        target = (me + s) % experts
        return copy(gg_out.at[target], gg_in.at[me], gg_send.at[s], gg_recv.at[me], expert=target)

    def gg_arrival(s):
        source = (me + s) % experts
        return copy(gg_out.at[source], gg_in.at[source], gg_send.at[s], gg_recv.at[source],
                    expert=source)

    for s in chip_hops:
        weight_send((chip + s) % chips * 2 + core, s).start()
    weight_send(partner, 0).start()

    earlier = jnp.where(
        lax.broadcasted_iota(jnp.int32, (rows, rows), 0)
        < lax.broadcasted_iota(jnp.int32, (rows, rows), 1), 1.0, 0.0).astype(BF16)
    places = lax.broadcasted_iota(jnp.int32, (cap, rows), 0)

    def picks_of(meta, e):
        first = (meta[0:1].astype(jnp.int32) == e).astype(F32)
        second = (meta[1:2].astype(jnp.int32) == e).astype(F32)
        member = jnp.broadcast_to(first + second, (8, rows))
        rank = dot(member.astype(BF16), earlier, ((1,), (0,)))
        hit = (rank[0:1].astype(jnp.int32) == places).astype(F32)
        return hit * first, hit * second

    def gate_rows(meta, one, two):
        return jnp.sum(one * meta[2:3] + two * meta[3:4], axis=1, keepdims=True)

    meta = meta_ref[...]
    for e in range(experts):
        one, two = picks_of(meta, e)
        pick_ref[e * cap:(e + 1) * cap, 0:rows] = one.astype(BF16)
        pick_ref[e * cap:(e + 1) * cap, rows:2 * rows] = two.astype(BF16)

    def home_picks(e):
        at = pl.ds(pl.multiple_of(e * cap, cap), cap)
        return pick_ref[at, 0:rows].astype(F32), pick_ref[at, rows:2 * rows].astype(F32)

    for i, target in enumerate(others + (me,)):
        one, two = home_picks(target)
        x_out[target] = dot(
            (one + two).astype(BF16), tokens_ref[...], ((1,), (0,))).astype(BF16)
        if i < 3:
            back_copy(0, i).start()
        else:
            x_in[me] = x_out[me]
    for i, target in enumerate(others + (me,)):
        one, two = home_picks(target)
        g_out[target] = (gate_rows(meta, one, two) * dot(
            (one + two).astype(BF16), cot_ref[...], ((1,), (0,)))).astype(BF16)
        if i < 3:
            back_copy(1, i).start()
        else:
            g_in[me] = g_out[me]

    def forward_weights(s):
        weight_arrival((chip + s) % chips * 2 + core).wait_recv()
        weight_forward(s).start()

    piece = 256

    for s in reversed(chip_hops):
        forward_weights(s)
    weight_arrival(partner).wait_recv()
    for s in reversed(chip_hops):
        weight_arrival((chip + s) % chips * 2 + 1 - core).wait_recv()
    for i in range(3):
        back_arrival(0, i).wait_recv()

    steps = 2
    per = experts // steps
    tall = per * cap

    @pl.loop(0, steps)
    def _(i):
        at = pl.ds(pl.multiple_of(i * tall, tall), tall)
        x = x_in[pl.ds(i * per, per)].reshape(tall, width)
        gate_pre = dot(x, weights[0], ((1,), (0,)))
        up_pre = dot(x, weights[1], ((1,), (0,)))
        gate_pre_ref[at, :] = gate_pre
        up_pre_ref[at, :] = up_pre
        hidden = (gate_pre * jax.nn.sigmoid(gate_pre) * up_pre).astype(BF16)
        hidden_ref[at, :] = hidden
        y_out[pl.ds(i * per, per)] = dot(hidden, weights[2], ((1,), (1,))).astype(BF16).reshape(
            per, cap, width)

    for i in range(3):
        back_copy(2, i).start()
    y_in[me] = y_out[me]

    for i in range(3):
        back_arrival(1, i).wait_recv()

    ones = jnp.ones((8, hidden_ref.shape[1]), BF16)

    @pl.loop(0, steps)
    def _(i):
        at = pl.ds(pl.multiple_of(i * tall, tall), tall)
        g = g_in[pl.ds(i * per, per)].reshape(tall, width)
        d_hidden = dot(g, weights[2], ((1,), (0,)))
        gate_pre = gate_pre_ref[at, :]
        up_pre = up_pre_ref[at, :]
        sigma = jax.nn.sigmoid(gate_pre)
        d_gate = (d_hidden * up_pre * sigma * (1.0 + gate_pre * (1.0 - sigma))).astype(BF16)
        d_up = (d_hidden * (gate_pre * sigma)).astype(BF16)
        d_gate_ref[at, :] = d_gate
        d_up_ref[at, :] = d_up
        entry = dot(d_gate, weights[0], ((1,), (1,))) + dot(d_up, weights[1], ((1,), (1,)))
        e_out[pl.ds(i * per, per)] = entry.astype(BF16).reshape(per, cap, width)
        product = hidden_ref[at, :].astype(F32) * d_hidden
        high = product.astype(BF16)
        low = (product - high.astype(F32)).astype(BF16)
        for j in range(per):
            cut = slice(j * cap, (j + 1) * cap)
            gg_out[i * per + j, :, 0:cap] = (
                dot(ones, high[cut], ((1,), (1,))) + dot(ones, low[cut], ((1,), (1,))))

    for s in gg_hops:
        gg_copy(s).start()
    for i in range(3):
        back_copy(3, i).start()
    e_in[me] = e_out[me]
    gg_in[me] = gg_out[me]

    @pl.loop(0, width // piece)
    def _(i):
        at = pl.ds(pl.multiple_of(i * piece, piece), piece)
        x = x_in[:, :, at].reshape(slots, piece)
        part[0, at, :] = dot(x, d_gate_ref[...], ((0,), (0,))).astype(BF16)
        part[1, at, :] = dot(x, d_up_ref[...], ((0,), (0,))).astype(BF16)
        g = g_in[:, :, at].reshape(slots, piece)
        part[2, at, :] = dot(g, hidden_ref[...], ((0,), (0,))).astype(BF16)

    def pair_send_of(s):
        target = (chip + s) % chips
        return copy(shard_of(part, target * 2 + 1 - core), pair_in.at[s],
                    pair_send.at[s], pair_recv.at[s], dp=partner)

    def share_send_of(s):
        return copy(summed.at[s], rs_in.at[s], rs_send.at[s], rs_recv.at[s],
                    dp=(chip + s) % chips * 2 + core)

    def own_sum(s):
        owner = (chip + s) % chips * 2 + core
        own = part[:, pl.ds(pl.multiple_of(owner * shard, shard), shard), :]
        return own.astype(F32) + pair_in[s].astype(F32)

    for s in chip_hops + [0]:
        pair_send_of(s).start()
    for s in chip_hops:
        pair_send_of(s).wait_recv()
        summed[s] = own_sum(s).astype(BF16)
        share_send_of(s).start()

    for s in gg_hops:
        gg_arrival(s).wait_recv()
    sums = jnp.zeros((8, 2 * rows), F32)
    for e in range(experts):
        row = gg_in[e, :, 0:cap]
        high = row.astype(BF16)
        low = (row - high.astype(F32)).astype(BF16)
        chosen = pick_ref[e * cap:(e + 1) * cap, :]
        sums += dot(high, chosen, ((1,), (0,))) + dot(low, chosen, ((1,), (0,)))
    gate_grads_ref[0:1, :] = sums[0:1, 0:rows] / meta_ref[2:3, :]
    gate_grads_ref[1:2, :] = sums[0:1, rows:2 * rows] / meta_ref[3:4, :]

    for i in range(3):
        back_arrival(2, i).wait_recv()

    @pl.loop(0, width // piece)
    def _(i):
        at = pl.ds(pl.multiple_of(i * piece, piece), piece)
        y = y_in[:, :, at].reshape(slots, piece)
        per_entry = dot(pick_ref[...], y, ((0,), (0,)))
        mixed_ref[:, at] = (
            gates_ref[:, 0:1] * per_entry[:rows] + gates_ref[:, 1:2] * per_entry[rows:]
        ).astype(BF16)

    pair_send_of(0).wait_recv()
    total = own_sum(0)
    for s in reversed(chip_hops):
        share_send_of(s).wait_recv()
        total += rs_in[s].astype(F32)
    share_g_ref[...] = total[0]
    share_u_ref[...] = total[1]
    share_d_ref[...] = total[2].T

    either = pick_ref[:, 0:rows] + pick_ref[:, rows:2 * rows]
    for i in range(3):
        back_arrival(3, i).wait_recv()

    @pl.loop(0, width // piece)
    def _(i):
        at = pl.ds(pl.multiple_of(i * piece, piece), piece)
        token_grads_ref[:, at] = dot(
            either, e_in[:, :, at].reshape(slots, piece), ((0,), (0,))).astype(BF16)

    for number in range(4):
        for i in range(3):
            back_copy(number, i).wait_send()
    for s in gg_hops:
        gg_copy(s).wait_send()
    for s in chip_hops:
        weight_send((chip + s) % chips * 2 + core, s).wait_send()
        weight_forward(s).wait_send()
        pair_send_of(s).wait_send()
        share_send_of(s).wait_send()
    weight_send(partner, 0).wait_send()
    pair_send_of(0).wait_send()


def line_body(tokens, routes, gates, cotangent, w_gate, w_up, w_down):
    experts = lax.axis_size("expert")
    groups = lax.axis_size("dp")
    rows, width = tokens.shape
    picks = routes.shape[1]
    hidden = w_gate.shape[2]
    shard = w_gate.shape[1]
    cap = max(2, 5 * rows * picks // (4 * experts))
    cap = -(-cap // 16) * 16
    lanes = -(-cap // 128) * 128
    slots = experts * cap
    chips = groups // 2
    meta = jnp.concatenate(
        [routes.T.astype(F32), gates.T, jnp.zeros((8 - 2 * picks, rows), F32)], axis=0)
    vmem = pl.BlockSpec(memory_space=pltpu.VMEM)
    dma = pltpu.SemaphoreType.DMA
    blocks = lambda *lead: pltpu.VMEM((*lead, cap, width), BF16)
    mixed, token_grads, gate_grads, share_g, share_u, share_d = pl.pallas_call(
        functools.partial(line_kernel, cap),
        out_shape=(
            jax.ShapeDtypeStruct((rows, width), BF16),
            jax.ShapeDtypeStruct((rows, width), BF16),
            jax.ShapeDtypeStruct((picks, rows), F32),
            jax.ShapeDtypeStruct((shard, hidden), F32),
            jax.ShapeDtypeStruct((shard, hidden), F32),
            jax.ShapeDtypeStruct((hidden, shard), F32),
        ),
        in_specs=[vmem] * 7,
        out_specs=(vmem,) * 6,
        scratch_shapes=[
            pltpu.VMEM((slots, picks * rows), BF16),
            blocks(experts), blocks(experts), blocks(experts), blocks(experts), blocks(experts), blocks(experts),
            blocks(experts), blocks(experts),
            pltpu.VMEM((experts, 8, lanes), F32), pltpu.VMEM((experts, 8, lanes), F32),
            pltpu.VMEM((3, width, hidden), BF16),
            pltpu.VMEM((slots, hidden), F32),
            pltpu.VMEM((slots, hidden), F32),
            pltpu.VMEM((slots, hidden), BF16),
            pltpu.VMEM((slots, hidden), BF16),
            pltpu.VMEM((slots, hidden), BF16),
            pltpu.VMEM((3, width, hidden), BF16),
            pltpu.VMEM((chips, 3, shard, hidden), BF16),
            pltpu.VMEM((chips, 3, shard, hidden), BF16),
            pltpu.VMEM((chips, 3, shard, hidden), BF16),
            dma((4, 3)), dma((4, experts)),
            dma((experts,)), dma((experts,)),
            dma((chips,)), dma((chips,)), dma((groups,)),
            dma((chips,)), dma((chips,)), dma((chips,)), dma((chips,)),
        ],
        compiler_params=pltpu.CompilerParams(
            collective_id=0, has_side_effects=True, vmem_limit_bytes=58 * 1024 * 1024
        ),
        name="routed_experts",
    )(tokens, cotangent, gates, meta, w_gate[0], w_up[0], w_down[0])
    return (mixed, token_grads, gate_grads.T, share_g[None], share_u[None], share_d[None])


def body(*arguments):
    in_line = lax.axis_size("expert") == 4 and arguments[4].shape[1] % 128 == 0
    return (line_body if in_line else direct_body)(*arguments)


def solution(mesh):
    return jax.shard_map(
        body,
        mesh=mesh,
        in_specs=(
            P(("dp", "expert"), None),
            P(("dp", "expert"), None),
            P(("dp", "expert"), None),
            P(("dp", "expert"), None),
            P("expert", "dp", None),
            P("expert", "dp", None),
            P("expert", None, "dp"),
        ),
        out_specs=(
            P(("dp", "expert"), None),
            P(("dp", "expert"), None),
            P(("dp", "expert"), None),
            P("expert", "dp", None),
            P("expert", "dp", None),
            P("expert", None, "dp"),
        ),
        check_vma=False,
    )
```
